512 devices in a mesh: seq: 64 (over z, y), head: 8 (over x, core).
Axes of the slice: x: 4, y: 4, z: 16, core: 2. Of those that a mesh axis runs over, the one named last changes fastest.
Arguments:
- queries: bfloat16 [32768, 4096], P(('seq', 'head')), may hold values from -8 to 8
- keys: bfloat16 [32768, 4096], P(('seq', 'head')), may hold values from -9 to 9
- values: bfloat16 [32768, 4096], P(('seq', 'head')), may hold values from -6 to 6
- grad_out: bfloat16 [32768, 4096], P(('seq', 'head')), may hold values from -6 to 6
- cluster_ids: int32 [32, 32768, 1], P('head', 'seq'), may hold values from 0 to 511; in each aligned block of 512 rows (0 to 511, 512 to 1023, ..., all dimensions but the last counted through in order) at most 2 rows name the same one
Outputs:
- attn_out: bfloat16 [32768, 4096], P(('seq', 'head'))
- query_gradient: bfloat16 [32768, 4096], P(('seq', 'head'))
- key_gradient: bfloat16 [32768, 4096], P(('seq', 'head'))
- value_gradient: bfloat16 [32768, 4096], P(('seq', 'head'))
The draws below stay inside these ranges and needn't reach their ends.
Inputs may be any that keep to these rules, and one draw needn't show every extreme that they name: `cluster_ids`: in each head, among the 512 tokens of one index of seq, no cluster is named more than 2 times, and in every draw some cluster is named exactly 2 times there.
All inputs are finite; a program needn't handle non-finite values.
Results may differ from the reference program's by a relative error of at most 0.015.
Values may be sent and summed in bfloat16 or wider, within the bound.
A program may use at most 64 MiB of HBM per device.

```python
import math
import jax
import jax.numpy as jnp
import numpy as np
from jax import lax

H = 32
HEAD_WIDTH = 128
CLUSTERS = 512
TOK_DEV = 512
MOST = 2
TOKENS = 32768
N_SEQ = 64


def draw_queries(key, part):
    base = jax.random.truncated_normal(jax.random.fold_in(key, 101), -4.0, 4.0, (TOKENS, H * HEAD_WIDTH), jnp.float32)
    return base.astype(jnp.bfloat16)


def draw_keys(key, part):
    base = jax.random.truncated_normal(jax.random.fold_in(key, 201), -4.0, 4.0, (TOKENS, H * HEAD_WIDTH), jnp.float32)
    return base.astype(jnp.bfloat16)


def levels(key, extent, pieces, least, top_value):
    def one(dim, blocks):
        steps = jax.random.uniform(jax.random.fold_in(jax.random.fold_in(key, 6), dim), (blocks,), jnp.float32, least / len(pieces), top_value / len(pieces))
        return jnp.repeat(jnp.exp(steps), extent[dim] // blocks).reshape((-1,) + (1,) * (len(extent) - dim - 1))

    factor_of = one(*pieces[0])
    for cut in pieces[1:]:
        factor_of = factor_of * one(*cut)
    return factor_of


def assign_block(own_key, own, number, rows, count, top, limit, lean):
    sequence = jax.random.permutation(own_key, count)
    heavy_load, ordinary = load_shares(count, rows * top, limit, lean, True), load_shares(count, rows * top, limit, lean, False)
    places = jnp.arange(count)

    def named(tallies, rotation):
        used = int((tallies > 0).sum())
        fixed = max(1, used // 4)
        passed = fixed + (places - fixed + rotation * (used - fixed)) % max(1, count - fixed)
        return jnp.zeros((count,), jnp.int32).at[sequence[jnp.where(places < fixed, places, passed)]].set(jnp.asarray(tallies, jnp.int32))

    tallies = jnp.where(number % 4 == 0, named(heavy_load, number // 4), named(ordinary, number - number // 4 - 1))
    mixed = jax.random.permutation(jax.random.fold_in(own, 3), count)
    donor, taker = mixed[0:count // 2 * 2:2], mixed[1:count // 2 * 2:2]
    slack = jnp.minimum(tallies[donor] - 1, limit - tallies[taker]) // 2
    slack = jnp.where((donor == sequence[0]) | (taker == sequence[0]) | (tallies[taker] == 0), 0, jnp.maximum(slack, 0))
    passed = jax.random.randint(jax.random.fold_in(own, 4), (count // 2,), 0, 1 << 20) % (slack + 1)
    tallies = tallies.at[donor].add(-passed).at[taker].add(passed)
    items = jnp.searchsorted(jnp.cumsum(tallies), jnp.arange(rows * top), side="right").astype(jnp.int32)
    listing = items.reshape(top, rows).T
    listing = listing[jax.random.permutation(jax.random.fold_in(own, 1), rows)]
    rotation = jax.random.randint(jax.random.fold_in(own, 2), (rows, 1), 0, top)
    return jnp.take_along_axis(listing, (jnp.arange(top)[None, :] + rotation) % top, axis=1)


def load_shares(amount, total, most, lean, full):
    loads = [(1 << 20) // math.isqrt(rank ** lean) + 1 for rank in range(1, amount + 1)]
    largest = most if full else min(most, max(-(-total // amount), total * loads[0] // sum(loads)))
    least = 1 if total - largest >= amount - 1 else 0
    holding, spare = [largest] + [least] * (amount - 1), total - largest - least * (amount - 1)
    while spare > 0:
        candidates = [i for i in range(1, amount) if holding[i] < largest] or [i for i in range(1, amount) if holding[i] < most]
        mass, budget = sum([loads[i] for i in candidates]), spare
        for i in candidates:
            more = min(most - holding[i], max(1, budget * loads[i] // mass), spare)
            holding[i] = holding[i] + more
            spare = spare - more
    return np.array(holding)


def centred(rng, shape, spread, limit, cuts=(), held_as=jnp.bfloat16):
    loudness = levels(rng, shape, cuts, -0.22, 0.18) if cuts else 1.0
    drawn = jax.random.normal(rng, shape, jnp.float32) * spread * loudness
    return jnp.minimum(jnp.maximum(drawn, -limit), limit).astype(held_as)


def setup_inputs(seed: int = 0) -> dict:
    splits = jax.random.split(jax.random.key(seed), 6)
    queries = draw_queries(jax.random.fold_in(splits[5], 71), 0)
    keys = draw_keys(jax.random.fold_in(splits[5], 71), 0)
    values = centred(splits[2], (TOKENS, H * HEAD_WIDTH), 1.0, 6.0, ((0, 512),))
    grad_out = centred(splits[3], (TOKENS, H * HEAD_WIDTH), 1.0, 6.0, ((0, 512),))
    cluster_ids_keys = jax.random.split(jax.random.fold_in(splits[4], 1), H * TOKENS // TOK_DEV)
    cluster_ids_turns = jax.random.permutation(jax.random.fold_in(splits[4], 3), H * TOKENS // TOK_DEV)
    cluster_ids = jax.vmap(lambda own, number: assign_block(jax.random.fold_in(splits[4], 2), own, number, TOK_DEV, CLUSTERS, 1, MOST, 2))(cluster_ids_keys, cluster_ids_turns).reshape((H, TOKENS, 1))
    return {"queries": queries, "keys": keys, "values": values, "grad_out": grad_out, "cluster_ids": cluster_ids}


def head_pass(args):
    qh, kh, vh, gh, ch = args
    scale = HEAD_WIDTH ** -0.5
    blocks = ch.reshape(N_SEQ, TOK_DEV).astype(jnp.int32)
    onehot = (blocks[:, :, None] == jnp.arange(CLUSTERS, dtype=jnp.int32)[None, None, :]).astype(jnp.int32)
    running = jnp.cumsum(onehot, axis=1)
    rank = jnp.sum(running * onehot, axis=2) - 1
    source = jnp.arange(N_SEQ, dtype=jnp.int32)[:, None]
    slots = N_SEQ * MOST
    target = (blocks * slots + source * MOST + rank).reshape(-1).astype(jnp.int32)
    total = CLUSTERS * slots

    def place(x):
        return jnp.zeros((total, HEAD_WIDTH), x.dtype).at[target].set(x).reshape(CLUSTERS, slots, HEAD_WIDTH)

    valid = jnp.zeros((total,), jnp.float32).at[target].set(1.0).reshape(CLUSTERS, slots)
    query_block = place(qh).astype(jnp.float32)
    key_block = place(kh).astype(jnp.float32)
    value_block = place(vh).astype(jnp.float32)
    output_gradient_block = place(gh).astype(jnp.float32)
    score = jnp.einsum('cqd,ckd->cqk', query_block, key_block) * scale
    score = jnp.where(valid[:, None, :] > 0, score, -1e30)
    top = jnp.max(score, axis=2, keepdims=True)
    expo = jnp.exp(score - top)
    probs = expo / jnp.sum(expo, axis=2, keepdims=True)
    probability_block = probs.astype(jnp.bfloat16).astype(jnp.float32)
    out = jnp.einsum('cqk,ckd->cqd', probability_block, value_block).astype(jnp.bfloat16)
    probability_gradient = jnp.einsum('cqd,ckd->cqk', output_gradient_block, value_block)
    score_gradient = probs * (probability_gradient - jnp.sum(probs * probability_gradient, axis=2, keepdims=True)) * scale
    score_gradient = score_gradient.astype(jnp.bfloat16).astype(jnp.float32)
    query_gradient = jnp.einsum('cqk,ckd->cqd', score_gradient, key_block).astype(jnp.bfloat16)
    key_gradient = jnp.einsum('cqk,cqd->ckd', score_gradient, query_block).astype(jnp.bfloat16)
    value_gradient = jnp.einsum('cqk,cqd->ckd', probability_block, output_gradient_block).astype(jnp.bfloat16)

    def pick(x):
        return x.reshape(total, HEAD_WIDTH)[target]

    return pick(out), pick(query_gradient), pick(key_gradient), pick(value_gradient)


def reference(queries, keys, values, grad_out, cluster_ids):
    def split(x):
        return x.reshape(TOKENS, H, HEAD_WIDTH).transpose(1, 0, 2)

    def merge(x):
        return x.transpose(1, 0, 2).reshape(TOKENS, H * HEAD_WIDTH)

    results = lax.map(head_pass, (split(queries), split(keys), split(values), split(grad_out), cluster_ids[:, :, 0]))
    return merge(results[0]), merge(results[1]), merge(results[2]), merge(results[3])
```

```python
import functools

import jax
import jax.numpy as jnp
from jax import lax
from jax.experimental import pallas as pl
from jax.experimental.pallas import tpu as pltpu
from jax.sharding import PartitionSpec as P

WIDTH = 128
CLUSTERS = 512
MOST = 2
TIGHT = 144
F32 = jnp.float32
BF16 = jnp.bfloat16
MESH = pl.DeviceIdType.MESH
BLOCK_Q = 256
NEG = -1e30


def iota(shape, dim):
    return lax.broadcasted_iota(jnp.int32, shape, dim)


def dot_nt(a, b):
    return lax.dot_general(a, b, (((1,), (1,)), ((), ())), preferred_element_type=F32)


def dot_tn(a, b):
    return lax.dot_general(a, b, (((0,), (0,)), ((), ())), preferred_element_type=F32)


def dot(a, b):
    return jnp.dot(a, b, preferred_element_type=F32)


def kernel(
    dims,
    q_ref, k_ref, v_ref, g_ref, ids_ref,
    out_ref, flag_ref,
    ids_buf, cnt_send, cnt_buf, flag_buf, rank_buf, pos_buf,
    rows, zsend, zrecv, zret, prob, marks, dk_acc, dv_acc,
    ids_sem, cnt_sem, flag_sem, one_sem, in_sem, back_sem, two_sem, own_sem,
):
    planes, lanes_y, groups, cap, per_dev = dims
    slots = planes * cap
    peers = lanes_y * groups
    seq_tok = groups * per_dev
    tokens = lanes_y * seq_tok
    chunks = tokens // 128
    per_seq = seq_tok // 128
    seq = lax.axis_index("seq")
    hd = lax.axis_index("head")
    z = seq // lanes_y
    y = seq % lanes_y
    mine = y * groups + hd

    def plane_peer(j):
        other_y = lax.rem(y + j // groups, lanes_y)
        other_h = lax.rem(hd + lax.rem(j, groups), groups)
        return other_y, other_h

    def plane_id(other_y, other_h):
        return (z * lanes_y + other_y, other_h)

    def ring_id(other_z):
        return (other_z * lanes_y + y, hd)

    barrier = pltpu.get_barrier_semaphore()

    @pl.loop(1, peers)
    def _(j):
        pl.semaphore_signal(barrier, inc=1, device_id=plane_id(*plane_peer(j)), device_id_type=MESH)

    @pl.loop(1, planes)
    def _(d):
        pl.semaphore_signal(
            barrier, inc=1, device_id=ring_id(lax.rem(z + d, planes)), device_id_type=MESH
        )

    pl.semaphore_wait(barrier, peers - 1 + planes - 1)

    @pl.loop(1, lanes_y)
    def _(d):
        other = lax.rem(y + d, lanes_y)
        pltpu.make_async_remote_copy(
            src_ref=ids_ref.at[other], dst_ref=ids_buf.at[y],
            send_sem=ids_sem.at[0], recv_sem=ids_sem.at[1],
            device_id=plane_id(other, hd), device_id_type=MESH,
        ).start()

    own_ids = pltpu.make_async_copy(ids_ref.at[y], ids_buf.at[y], own_sem.at[4])
    own_ids.start()

    own_copies = []
    for ti, ref in enumerate((q_ref, k_ref, v_ref, g_ref)):

        @pl.loop(1, peers)
        def _(j, ti=ti, ref=ref):
            other_y, other_h = plane_peer(j)
            head = other_h * lanes_y + other_y
            pltpu.make_async_remote_copy(
                src_ref=ref.at[:, pl.ds(pl.multiple_of(head * WIDTH, WIDTH), WIDTH)],
                dst_ref=rows.at[ti, pl.ds(pl.multiple_of(mine * per_dev, per_dev), per_dev), :],
                send_sem=one_sem.at[0, ti], recv_sem=one_sem.at[1, ti],
                device_id=plane_id(other_y, other_h), device_id_type=MESH,
            ).start()

        head = hd * lanes_y + y
        copy = pltpu.make_async_copy(
            ref.at[:, pl.ds(pl.multiple_of(head * WIDTH, WIDTH), WIDTH)],
            rows.at[ti, pl.ds(pl.multiple_of(mine * per_dev, per_dev), per_dev), :],
            own_sem.at[ti],
        )
        copy.start()
        own_copies.append(copy)

    def drain(ref, sem):
        pltpu.make_async_copy(ref, ref, sem).wait()

    own_ids.wait()
    drain(ids_buf.at[pl.ds(0, lanes_y - 1)], ids_sem.at[1])

    tri = jnp.where(iota((128, 128), 0) <= iota((128, 128), 1), 1.0, 0.0).astype(BF16)
    full = jnp.ones((128, 128), BF16)
    tri_full = jnp.concatenate([tri, full], axis=1)
    eye = iota((128, 128), 0) == iota((128, 128), 1)

    def ids_row(ch):
        return ids_buf[ch // per_seq, pl.ds(lax.rem(ch, per_seq), 1), :]

    def rank_step(ch, carry):
        member = iota((CLUSTERS, 128), 0) == ids_row(ch)
        both = dot(jnp.where(member, 1.0, 0.0).astype(BF16), tri_full)
        rank = jnp.sum(
            jnp.where(member, both[:, :128] + carry - 1.0, 0.0), axis=0, keepdims=True
        )
        rank_buf[pl.ds(ch, 1), :] = rank
        return carry + both[:, 128:]

    sizes = lax.fori_loop(0, chunks, rank_step, jnp.zeros((CLUSTERS, 128), F32))

    def col_to_row(col):
        return jnp.concatenate(
            [
                jnp.sum(jnp.where(eye, col[i:i + 128, :], 0.0), axis=0, keepdims=True)
                for i in range(0, CLUSTERS, 128)
            ],
            axis=1,
        )

    def row_to_col(row):
        return jnp.concatenate(
            [
                jnp.sum(jnp.where(eye, row[:, i:i + 128], 0.0), axis=1, keepdims=True)
                for i in range(0, row.shape[1], 128)
            ],
            axis=0,
        )

    size_row = col_to_row(sizes)
    cnt_send[...] = size_row
    cnt_buf[z] = size_row

    @pl.loop(1, planes)
    def _(d):
        pltpu.make_async_remote_copy(
            src_ref=cnt_send, dst_ref=cnt_buf.at[z],
            send_sem=cnt_sem.at[0], recv_sem=cnt_sem.at[1],
            device_id=ring_id(lax.rem(z + d, planes)), device_id_type=MESH,
        ).start()

    drain(cnt_buf.at[pl.ds(0, planes - 1)], cnt_sem.at[1])
    drain(cnt_buf.at[pl.ds(0, planes - 1)], cnt_sem.at[0])

    counts = jnp.concatenate([cnt_buf[i] for i in range(planes)], axis=0)
    total = jnp.sum(counts, axis=0, keepdims=True)
    total_col = row_to_col(total)
    sub = iota((CLUSTERS, CLUSTERS), 0)
    lane = iota((CLUSTERS, CLUSTERS), 1)
    ahead = jnp.where(
        (total_col > total) | ((total_col == total) & (sub < lane)), 1.0, 0.0
    )
    order = jnp.sum(ahead, axis=0, keepdims=True)
    order_col = row_to_col(order)
    perm = order_col.astype(jnp.int32) == lane

    def owner_of(r):
        turn = lax.rem(r, 2 * planes)
        return jnp.where(turn < planes, turn, 2 * planes - 1 - turn)

    sorted_counts = dot(counts.astype(BF16), jnp.where(perm, 1.0, 0.0).astype(BF16))
    before = jnp.where((sub < lane) & (owner_of(sub) == owner_of(lane)), 1.0, 0.0)
    offset = dot(sorted_counts.astype(BF16), before.astype(BF16))
    over = jnp.where(offset + sorted_counts > cap, 1.0, 0.0)
    over = jnp.max(jnp.max(over, axis=0, keepdims=True), axis=1, keepdims=True)
    over = jnp.broadcast_to(over, (1, 128))
    flag_ref[...] = over
    flag_buf[mine] = over

    own_offset = jnp.sum(
        jnp.where(iota((planes, CLUSTERS), 0) == z, offset, 0.0), axis=0, keepdims=True
    )
    start_row = own_offset + (owner_of(iota((1, CLUSTERS), 1)) * cap).astype(F32)
    start_col = jnp.sum(jnp.where(perm, start_row, 0.0), axis=1, keepdims=True)

    def pos_step(ch, carry):
        member = iota((CLUSTERS, 128), 0) == ids_row(ch)
        base = jnp.sum(jnp.where(member, start_col, 0.0), axis=0, keepdims=True)
        pos_buf[pl.ds(ch, 1), :] = (base + rank_buf[pl.ds(ch, 1), :]).astype(jnp.int32)
        return carry

    lax.fori_loop(0, chunks, pos_step, 0)
    pos = jnp.concatenate([pos_buf[i:i + 1, :] for i in range(chunks)], axis=1)

    step = 4 if planes % 4 == 0 else 1

    def pack_step(b, ti):
        parts = []
        for j in range(step):
            dest = lax.rem(z + b * step + j, planes)
            parts.append(
                jnp.where(iota((cap, tokens), 0) + dest * cap == pos, 1.0, 0.0).astype(BF16)
            )
        packed = dot(jnp.concatenate(parts, axis=0), rows[ti]).astype(BF16)
        for j in range(step):
            dest = lax.rem(z + b * step + j, planes)
            at = pl.ds(pl.multiple_of(dest * cap, cap), cap)
            zsend[ti, at, :] = packed[j * cap:(j + 1) * cap]
            to = pl.ds(pl.multiple_of(z * cap, cap), cap)

            @pl.when(dest != z)
            def _(dest=dest, at=at, to=to):
                pltpu.make_async_remote_copy(
                    src_ref=zsend.at[ti, at, :], dst_ref=zrecv.at[ti, to, :],
                    send_sem=in_sem.at[0, ti], recv_sem=in_sem.at[1, ti],
                    device_id=ring_id(dest), device_id_type=MESH,
                ).start()

            @pl.when(dest == z)
            def _(j=j, to=to):
                zrecv[ti, to, :] = packed[j * cap:(j + 1) * cap]

        return ti

    for ti in range(4):
        own_copies[ti].wait()
        drain(rows.at[ti, pl.ds(0, (peers - 1) * per_dev), :], one_sem.at[1, ti])
        lax.fori_loop(0, planes // step, pack_step, ti)


    @pl.loop(1, peers)
    def _(j):
        pltpu.make_async_remote_copy(
            src_ref=flag_ref, dst_ref=flag_buf.at[mine],
            send_sem=flag_sem.at[0], recv_sem=flag_sem.at[1],
            device_id=plane_id(*plane_peer(j)), device_id_type=MESH,
        ).start()

    lane_l = iota((CLUSTERS, 128), 1)
    sub_l = iota((CLUSTERS, 128), 0)
    chosen = jnp.where((sub_l // planes == lane_l) & (owner_of(sub_l) == z), 1.0, 0.0).astype(BF16)
    first = dot(offset.astype(BF16), chosen).astype(jnp.int32)
    length = dot(sorted_counts.astype(BF16), chosen).astype(jnp.int32)
    slot = iota((cap, 128), 0)
    for i in range(planes):
        low = first[i:i + 1, :]
        mark = (slot >= low) & (slot < low + length[i:i + 1, :])
        marks[i * cap:(i + 1) * cap, :] = jnp.where(mark, 1.0, 0.0).astype(BF16)

    received = pl.ds(0, (planes - 1) * cap)
    scale = WIDTH ** -0.5
    blocks = slots // BLOCK_Q

    def rows_of(b):
        return pl.ds(pl.multiple_of(b * BLOCK_Q, BLOCK_Q), BLOCK_Q)

    drain(zrecv.at[0, received, :], in_sem.at[1, 0])
    drain(zrecv.at[1, received, :], in_sem.at[1, 1])

    @pl.loop(0, blocks)
    def _(b):
        at = rows_of(b)
        score = dot_nt(zrecv[0, at, :], zrecv[1]) * scale
        same = dot_nt(marks[at, :], marks[...])
        score = jnp.where(same > 0.5, score, NEG)
        top = jnp.max(score, axis=1, keepdims=True)
        expo = jnp.exp(score - top)
        prob[at, :] = (expo / jnp.sum(expo, axis=1, keepdims=True)).astype(BF16)

    drain(zrecv.at[2, received, :], in_sem.at[1, 2])
    drain(zrecv.at[0, received, :], in_sem.at[0, 0])

    @pl.loop(0, blocks)
    def _(b):
        at = rows_of(b)
        zsend[0, at, :] = dot(prob[at, :], zrecv[2]).astype(BF16)

    def give_back(ti):
        at = pl.ds(pl.multiple_of(z * cap, cap), cap)

        @pl.loop(1, planes)
        def _(d):
            dest = lax.rem(z + d, planes)
            pltpu.make_async_remote_copy(
                src_ref=zsend.at[ti, pl.ds(pl.multiple_of(dest * cap, cap), cap), :],
                dst_ref=zret.at[ti, at, :],
                send_sem=back_sem.at[0, ti], recv_sem=back_sem.at[1, ti],
                device_id=ring_id(dest), device_id_type=MESH,
            ).start()

        zret[ti, at, :] = zsend[ti, at, :]

    give_back(0)
    for ti in range(1, 4):
        drain(zrecv.at[ti, received, :], in_sem.at[0, ti])
    drain(zrecv.at[3, received, :], in_sem.at[1, 3])

    dk_acc[...] = jnp.zeros_like(dk_acc)
    dv_acc[...] = jnp.zeros_like(dv_acc)

    @pl.loop(0, blocks)
    def _(b):
        at = rows_of(b)
        grad = zrecv[3, at, :]
        part = prob[at, :]
        wide = part.astype(F32)
        dprob = dot_nt(grad, zrecv[2])
        mean = jnp.sum(wide * dprob, axis=1, keepdims=True)
        dscore = (wide * (dprob - mean) * scale).astype(BF16)
        zsend[1, at, :] = dot(dscore, zrecv[1]).astype(BF16)
        dk_acc[...] += dot_tn(dscore, zrecv[0, at, :])
        dv_acc[...] += dot_tn(part, grad)

    give_back(1)
    zsend[2] = dk_acc[...].astype(BF16)
    give_back(2)
    zsend[3] = dv_acc[...].astype(BF16)
    give_back(3)

    for ti in range(4):
        drain(rows.at[ti, pl.ds(0, (peers - 1) * per_dev), :], one_sem.at[0, ti])

    batch = 256 // per_dev if per_dev < 256 else 1
    span = batch * per_dev
    own_cols = pl.ds(pl.multiple_of((hd * lanes_y + y) * WIDTH, WIDTH), WIDTH)

    for ti in range(4):
        drain(zret.at[ti, received, :], back_sem.at[1, ti])

        @pl.loop(0, tokens // span)
        def _(b, ti=ti):
            cols = []
            for i in range(span // 128):
                row = pos_buf[pl.ds(b * (span // 128) + i, 1), :].astype(F32)
                cols.append(jnp.sum(jnp.where(eye, row, 0.0), axis=1, keepdims=True))
            place = jnp.concatenate(cols, axis=0).astype(jnp.int32)
            pick = jnp.where(iota((span, slots), 1) == place, 1.0, 0.0).astype(BF16)
            at = pl.ds(pl.multiple_of(b * span, span), span)
            rows[ti, at, :] = dot(pick, zret[ti]).astype(BF16)
            for j in range(batch):
                index = b * batch + j
                source = rows.at[ti, pl.ds(pl.multiple_of(index * per_dev, per_dev), per_dev), :]

                @pl.when(index != mine)
                def _(index=index, source=source):
                    pltpu.make_async_remote_copy(
                        src_ref=source, dst_ref=out_ref.at[ti, :, own_cols],
                        send_sem=two_sem.at[0, ti], recv_sem=two_sem.at[1, ti],
                        device_id=plane_id(index // groups, lax.rem(index, groups)),
                        device_id_type=MESH,
                    ).start()

                @pl.when(index == mine)
                def _(source=source):
                    pltpu.make_async_copy(
                        source, out_ref.at[ti, :, own_cols], own_sem.at[ti]
                    ).start()

    drain(flag_buf.at[pl.ds(0, peers - 1)], flag_sem.at[1])
    drain(flag_buf.at[pl.ds(0, peers - 1)], flag_sem.at[0])
    flags = flag_buf[0]
    for i in range(1, peers):
        flags = jnp.maximum(flags, flag_buf[i])
    flag_ref[...] = flags
    drain(ids_buf.at[pl.ds(0, lanes_y - 1)], ids_sem.at[0])
    for ti in range(4):
        drain(zrecv.at[ti, received, :], back_sem.at[0, ti])
        own = rows.at[ti, pl.ds(0, per_dev), :]
        drain(own, own_sem.at[ti])
        plane_rows = rows.at[ti, pl.ds(0, (peers - 1) * per_dev), :]
        drain(plane_rows, two_sem.at[0, ti])
        drain(plane_rows, two_sem.at[1, ti])


def attend(cap, planes, lanes_y, groups, queries, keys, values, grad_out, ids):
    per_dev = queries.shape[0]
    tokens = lanes_y * groups * per_dev
    slots = planes * cap
    dma = pltpu.SemaphoreType.DMA
    chunk_rows = tokens // 128
    return pl.pallas_call(
        functools.partial(kernel, (planes, lanes_y, groups, cap, per_dev)),
        out_shape=(
            jax.ShapeDtypeStruct((4,) + queries.shape, BF16),
            jax.ShapeDtypeStruct((1, 128), F32),
        ),
        in_specs=[pl.BlockSpec(memory_space=pl.ANY)] * 5,
        out_specs=(
            pl.BlockSpec(memory_space=pl.ANY),
            pl.BlockSpec(memory_space=pltpu.VMEM),
        ),
        scratch_shapes=[
            pltpu.VMEM(ids.shape, jnp.int32),
            pltpu.VMEM((1, CLUSTERS), F32),
            pltpu.VMEM((planes, 1, CLUSTERS), F32),
            pltpu.VMEM((lanes_y * groups, 1, 128), F32),
            pltpu.VMEM((chunk_rows, 128), F32),
            pltpu.VMEM((chunk_rows, 128), jnp.int32),
            pltpu.VMEM((4, tokens, WIDTH), BF16),
            pltpu.VMEM((4, slots, WIDTH), BF16),
            pltpu.VMEM((4, slots, WIDTH), BF16),
            pltpu.VMEM((4, slots, WIDTH), BF16),
            pltpu.VMEM((slots, slots), BF16),
            pltpu.VMEM((slots, 128), BF16),
            pltpu.VMEM((slots, WIDTH), F32),
            pltpu.VMEM((slots, WIDTH), F32),
            dma((2,)), dma((2,)), dma((2,)),
            dma((2, 4)), dma((2, 4)), dma((2, 4)), dma((2, 4)),
            dma((6,)),
        ],
        compiler_params=pltpu.CompilerParams(
            collective_id=1 if cap == TIGHT else 2,
            has_side_effects=True,
            vmem_limit_bytes=66_000_000,
        ),
        name="attend_%d" % cap,
    )(queries, keys, values, grad_out, ids)


def solution(mesh):
    seq_count, groups = mesh.shape["seq"], mesh.shape["head"]

    def body(queries, keys, values, grad_out, cluster_ids):
        lanes_y, seq_tok = cluster_ids.shape[0], cluster_ids.shape[1]
        planes = seq_count // lanes_y
        loose = lanes_y * MOST * CLUSTERS // planes
        ids = cluster_ids.reshape(lanes_y, seq_tok // 128, 128)
        arrays = (queries, keys, values, grad_out, ids)
        out, flag = attend(TIGHT, planes, lanes_y, groups, *arrays)
        out = lax.cond(
            flag[0, 0] > 0.5,
            lambda: attend(loose, planes, lanes_y, groups, *arrays)[0],
            lambda: out,
        )
        return out[0], out[1], out[2], out[3]

    row_spec = P(("seq", "head"), None)
    return jax.shard_map(
        body,
        mesh=mesh,
        in_specs=(row_spec,) * 4 + (P("head", "seq", None),),
        out_specs=(row_spec,) * 4,
        check_vma=False,
    )
```
